32 devices in a mesh: seq: 16 (over z, y, core), head: 2 (over x).
Axes of the slice: x: 2, y: 2, z: 4, core: 2. Of those that a mesh axis runs over, the one named last changes fastest.
Arguments:
- query: bfloat16 [2048, 2048], P('seq', 'head'), may hold values from -0.47851562 to 0.47851562
- key: bfloat16 [2048, 2048], P('seq', 'head'), may hold values from -0.47851562 to 0.47851562
- value: bfloat16 [2048, 2048], P('seq', 'head'), may hold values from -0.47851562 to 0.47851562
- result_sensitivity: bfloat16 [2048, 2048], P('seq', 'head'), may hold values from -6 to 6
- w_value: bfloat16 [4096, 2048], P('head'), may hold values from -0.125 to 0.125
Outputs:
- query_grad: bfloat16 [2048, 2048], P('seq', 'head')
- key_grad: bfloat16 [2048, 2048], P('seq', 'head')
- value_grad: bfloat16 [2048, 2048], P('seq', 'head')
- input_grad: bfloat16 [2048, 4096], P('seq', 'head')
The draws below stay inside these ranges and needn't reach their ends.
All inputs are finite; a program needn't handle non-finite values.
Results may differ from the reference program's by a relative error of at most 0.0057.
Values may be sent and summed in bfloat16 or wider, within the bound.
No kernel may reach another device: no remote copies, remote signals or barrier semaphores. Data moves between devices by JAX's collectives and lax.ppermute only.
A program may use at most 64 MiB of HBM per device.

```python
import jax
import jax.numpy as jnp
from jax import lax

D = 4096
HEADS = 16
DH = 128
TOK_DEV = 128
TOKENS = 2048


def block_levels(rng, extent, cuts, low, high):
    loudness = 1.0
    for axis_at, parts in cuts:
        draws = jax.random.uniform(jax.random.fold_in(jax.random.fold_in(rng, 6), axis_at), (parts,), jnp.float32, low / len(cuts), high / len(cuts))
        loudness = loudness * jnp.repeat(jnp.exp(draws), extent[axis_at] // parts).reshape((-1,) + (1,) * (len(extent) - 1 - axis_at))
    return loudness


def gaussian(stream_key, extent, spread, bound, cuts=(), held_as=jnp.bfloat16):
    result = jax.random.normal(stream_key, extent, jnp.float32) * spread
    if len(cuts) > 0:
        result = block_levels(stream_key, extent, cuts, -0.22, 0.18) * result
    return jnp.clip(result, min=-bound, max=bound).astype(held_as)


def setup_inputs(seed: int = 0) -> dict:
    key_list = jax.random.split(jax.random.key(seed), 6)
    query = gaussian(key_list[0], (TOKENS, HEADS * DH), 0.08, 0.47851562, ((0, 16), (1, 2)))
    key = gaussian(key_list[1], (TOKENS, HEADS * DH), 0.08, 0.47851562, ((0, 16), (1, 2)))
    value = gaussian(key_list[2], (TOKENS, HEADS * DH), 0.08, 0.47851562, ((0, 16), (1, 2)))
    result_sensitivity = gaussian(key_list[3], (TOKENS, HEADS * DH), 1.0, 6.0, ((0, 16), (1, 2)))
    w_value = gaussian(key_list[4], (D, HEADS * DH), (HEADS * DH) ** -0.5, 0.125, ((0, 2),))
    return {"query": query, "key": key, "value": value, "result_sensitivity": result_sensitivity, "w_value": w_value}


def reference(query, key, value, result_sensitivity, w_value):
    blocks = TOKENS // TOK_DEV
    q_all = query.astype(jnp.float32).reshape(blocks, TOK_DEV, HEADS, DH)
    k_all = key.astype(jnp.float32).reshape(blocks, TOK_DEV, HEADS, DH)
    v_all = value.astype(jnp.float32).reshape(blocks, TOK_DEV, HEADS, DH)
    g_all = result_sensitivity.astype(jnp.float32).reshape(blocks, TOK_DEV, HEADS, DH)
    key_value_inside = jnp.einsum('bthk,bthv->bhkv', k_all, v_all)
    query_gradient_inside = jnp.einsum('bthk,bthv->bhkv', q_all, g_all)
    outer_running_inclusive = jnp.cumsum(key_value_inside, axis=0)
    leading_state = (outer_running_inclusive - key_value_inside).astype(jnp.bfloat16)
    qg_incl = jnp.cumsum(query_gradient_inside[::-1], axis=0)[::-1]
    trailing_state = (qg_incl - query_gradient_inside).astype(jnp.bfloat16)
    causal = jnp.tril(jnp.ones((TOK_DEV, TOK_DEV), jnp.float32))

    def one_block(items):
        query_block, lookup_segment, value_block, result_sensitivity_segment, running_accumulator, suffix_carry = items
        running_accumulator = running_accumulator.astype(jnp.float32)
        suffix_carry = suffix_carry.astype(jnp.float32)
        score_matrix = (jnp.einsum('thk,shk->hts', query_block, lookup_segment) * causal).astype(jnp.bfloat16).astype(jnp.float32)
        derivative_triple = (jnp.einsum('thv,shv->hts', result_sensitivity_segment, value_block) * causal).astype(jnp.bfloat16).astype(jnp.float32)
        probe_derivative = jnp.einsum('gzj,jgy->zgy', derivative_triple, lookup_segment) + jnp.einsum('wlh,lih->wli', result_sensitivity_segment, running_accumulator)
        key_gradient = jnp.einsum('rbp,brf->prf', derivative_triple, query_block) + jnp.einsum('qag,amg->qam', value_block, suffix_carry)
        value_gradient = jnp.einsum('yoj,oyg->jyg', score_matrix, result_sensitivity_segment) + jnp.einsum('plq,lqx->plx', lookup_segment, suffix_carry)
        return probe_derivative.astype(jnp.bfloat16), key_gradient.astype(jnp.bfloat16), value_gradient.astype(jnp.bfloat16)

    probe_derivative, key_gradient, value_gradient = lax.map(one_block, (q_all, k_all, v_all, g_all, leading_state, trailing_state))
    query_grad = probe_derivative.reshape(TOKENS, HEADS * DH)
    key_grad = key_gradient.reshape(TOKENS, HEADS * DH)
    value_grad = value_gradient.reshape(TOKENS, HEADS * DH)
    input_grad = lax.dot_general(value_grad, w_value, (((1,), (1,)), ((), ())), preferred_element_type=jnp.float32).astype(jnp.bfloat16)
    return query_grad, key_grad, value_grad, input_grad
```

```python
import functools

import jax
import jax.numpy as jnp
from jax import lax
from jax.experimental import pallas as pl
from jax.experimental.pallas import tpu as pltpu
from jax.sharding import PartitionSpec as P

DH = 128
BF = jnp.bfloat16
F32 = jnp.float32
VMEM = pl.BlockSpec(memory_space=pltpu.VMEM)
SMEM = pl.BlockSpec(memory_space=pltpu.SMEM)
HBM = pl.BlockSpec(memory_space=pl.ANY)


def dot(a, b, ca, cb):
    return lax.dot_general(a, b, (((ca,), (cb,)), ((), ())), preferred_element_type=F32)


def head_cols(ref, h):
    if isinstance(h, int):
        return ref[:, h * DH : (h + 1) * DH]
    return ref[:, pl.ds(pl.multiple_of(h * DH, DH), DH)]


def local_states(pos_ref, q_ref, k_ref, v_ref, g_ref, keep_ref, give_ref, whole_ref):
    core = pos_ref[0]
    half = keep_ref.shape[1]
    for j in range(half):
        for owner, out in ((1 - core, give_ref), (core, keep_ref)):
            h = owner * half + j
            qg = dot(head_cols(q_ref, h), head_cols(g_ref, h), 0, 0)
            kv = dot(head_cols(k_ref, h), head_cols(v_ref, h), 0, 0)
            out[0, j] = kv.astype(out.dtype)
            out[1, j] = qg.astype(out.dtype)
            whole_ref[h] = jnp.where(core == 0, kv, qg).astype(BF)


def inside_block(pos_ref, q_ref, k_ref, v_ref, g_ref, near_ref, dq_ref, dk_ref, dv_ref, sent_ref):
    core = pos_ref[0]
    rows = q_ref.shape[0]
    t = lax.broadcasted_iota(jnp.int32, (rows, rows), 0)
    s = lax.broadcasted_iota(jnp.int32, (rows, rows), 1)
    causal = s <= t
    for h in range(near_ref.shape[0]):
        cols = slice(h * DH, (h + 1) * DH)
        q, k, v, g = q_ref[:, cols], k_ref[:, cols], v_ref[:, cols], g_ref[:, cols]
        near = near_ref[h]
        near_kv = jnp.where(core == 1, near, jnp.zeros_like(near))
        near_qg = jnp.where(core == 0, near, jnp.zeros_like(near))
        scores = jnp.where(causal, dot(q, k, 1, 1), 0.0).astype(BF)
        grads = jnp.where(causal, dot(g, v, 1, 1), 0.0).astype(BF)
        dq_ref[:, cols] = dot(grads, k, 1, 0) + dot(g, near_kv, 1, 1)
        dk_ref[:, cols] = dot(grads, q, 0, 0) + dot(v, near_qg, 1, 1)
        dv = dot(scores, g, 0, 0) + dot(k, near_qg, 1, 0)
        dv_ref[:, cols] = dv
        sent_ref[:, cols] = dv.astype(BF)


def finish(parts, pos_ref, *refs):
    k_ref, v_ref, g_ref, dq_ref, dk_ref, dv_ref, w_ref = refs[:7]
    others = [refs[7 + 2 * i : 9 + 2 * i] for i in range(parts - 1)]
    at = 7 + 2 * (parts - 1)
    far_kv = refs[at : at + 4]
    far_qg = [refs[at + 4 + 4 * i : at + 8 + 4 * i] for i in range(parts)]
    at += 4 + 4 * parts
    qo, ko, vo, io, full, qs, ks, vs, os, sem = refs[at:]
    core, yy, x = pos_ref[0], pos_ref[1], pos_ref[2]
    quarter = far_kv[0].shape[0]
    width = k_ref.shape[1]
    ready = []
    for i in range(parts):
        x_from = lax.rem(x - i + parts, parts)
        kk, base = (k_ref, dv_ref) if i == 0 else others[i - 1]
        for piece in range(4):
            cc, dy = piece // 2, piece % 2
            first = ((core + cc) % 2 * 2 + (yy + dy) % 2) * quarter
            for j in range(quarter):
                h = first + j
                dv = head_cols(base, h).astype(F32) + dot(head_cols(kk, h), far_qg[i][piece][j], 1, 0)
                dv = dv.astype(BF)
                full[:, pl.ds(pl.multiple_of(x_from * width + h * DH, DH), DH)] = dv
                if i == 0:
                    vs[:, pl.ds(pl.multiple_of(h * DH, DH), DH)] = dv
    copies = [pltpu.make_async_copy(vs, vo, sem.at[0])]
    copies[0].start()
    features = w_ref.shape[0]
    step = min(512, features)
    for f in range(0, features, step):
        os[:, f : f + step] = dot(full[...], w_ref[f : f + step, :], 1, 1).astype(BF)
        cp = pltpu.make_async_copy(os.at[:, f : f + step], io.at[:, f : f + step], sem.at[3 + f // step])
        cp.start()
        copies.append(cp)
    for piece in range(4):
        cc, dy = piece // 2, piece % 2
        first = ((core + cc) % 2 * 2 + (yy + dy) % 2) * quarter
        for j in range(quarter):
            h = first + j
            cols = pl.ds(pl.multiple_of(h * DH, DH), DH)
            ks[:, cols] = (dk_ref[:, cols] + dot(v_ref[:, cols], far_qg[0][piece][j], 1, 1)).astype(BF)
            qs[:, cols] = (dq_ref[:, cols] + dot(g_ref[:, cols], far_kv[piece][j], 1, 1)).astype(BF)
    for n, (a, b) in enumerate(((qs, qo), (ks, ko))):
        cp = pltpu.make_async_copy(a, b, sem.at[1 + n])
        cp.start()
        copies.append(cp)
    for cp in copies:
        cp.wait()


def swap(value, bit):
    n = lax.axis_size("seq")
    return lax.ppermute(value, "seq", [(i, i ^ bit) for i in range(n)])


def hand(value, dx, bit):
    n, m = lax.axis_size("seq"), lax.axis_size("head")
    pairs = [(s * m + x, (s ^ bit) * m + (x + dx) % m) for s in range(n) for x in range(m)]
    return lax.ppermute(value, ("seq", "head"), pairs)


def across_groups(kv, qg, group):
    n = lax.axis_size("seq")
    groups = n // group
    mine = lax.axis_index("seq") // group
    rounds = (groups - 1).bit_length()
    if groups & (groups - 1) == 0 and groups - 1 <= 2 * rounds:
        kv_sum, qg_sum = jnp.zeros_like(kv), jnp.zeros_like(qg)
        kv16, qg16 = kv.astype(BF), qg.astype(BF)
        arrived = []
        for d in range(1, groups):
            sent = jnp.where((mine ^ d) > mine, kv16, qg16)
            arrived.append((d, swap(sent, d * group)))
        for d, got in arrived:
            got = got.astype(F32)
            below = (mine ^ d) < mine
            kv_sum = kv_sum + jnp.where(below, got, 0.0)
            qg_sum = qg_sum + jnp.where(below, 0.0, got)
        return kv_sum, qg_sum
    up = lambda a, by: lax.ppermute(a.astype(BF), "seq", [(i, i + by) for i in range(n - by)]).astype(F32)
    down = lambda a, by: lax.ppermute(a.astype(BF), "seq", [(i + by, i) for i in range(n - by)]).astype(F32)
    kv_sum, qg_sum = up(kv, group), down(qg, group)
    reach = 1
    while reach < groups:
        kv_sum = kv_sum + up(kv_sum, reach * group)
        qg_sum = qg_sum + down(qg_sum, reach * group)
        reach *= 2
    return kv_sum, qg_sum


def per_device(query, key, value, sensitivity, w_value):
    rows, width = query.shape
    heads = width // DH
    half, quarter = heads // 2, heads // 4
    parts = lax.axis_size("head")
    seq = lax.axis_index("seq")
    core, yy = seq % 2, (seq // 2) % 2
    pos = jnp.stack([core, yy, lax.axis_index("head")]).astype(jnp.int32)
    st = lambda *s, d=BF: jax.ShapeDtypeStruct(s, d)
    mm = 2 * rows * DH * DH

    keep, give, whole = pl.pallas_call(
        local_states,
        out_shape=(st(2, half, DH, DH, d=F32), st(2, half, DH, DH), st(heads, DH, DH)),
        in_specs=[SMEM] + [VMEM] * 4,
        out_specs=[VMEM] * 3,
        name="local_states",
        cost_estimate=pl.CostEstimate(flops=2 * heads * mm, bytes_accessed=8 * rows * width, transcendentals=0),
    )(pos, query, key, value, sensitivity)

    key_others = [hand(key, d, 0) for d in range(1, parts)]
    chip = keep + swap(give, 1).astype(F32)
    near = swap(whole, 1)

    split = chip.reshape(2, 2, quarter, DH, DH)
    chip_mine = jnp.where(yy == 0, split[:, 0], split[:, 1])
    chip_give = jnp.where(yy == 0, split[:, 1], split[:, 0]).astype(BF)
    chip_other = swap(chip_give, 2).astype(F32)

    dq, dk, dv, dv16 = pl.pallas_call(
        inside_block,
        out_shape=(st(rows, width, d=F32),) * 3 + (st(rows, width),),
        in_specs=[SMEM] + [VMEM] * 5,
        out_specs=[VMEM] * 4,
        name="inside_block",
        cost_estimate=pl.CostEstimate(flops=8 * heads * mm, bytes_accessed=8 * rows * width, transcendentals=0),
    )(pos, query, key, value, sensitivity, near)
    dv_others = [hand(dv16, d, 0) for d in range(1, parts)]

    both = chip_mine + chip_other
    kv_far, qg_far = across_groups(both[0], both[1], 4)
    first, second = jnp.where(yy == 0, chip_mine, chip_other), jnp.where(yy == 0, chip_other, chip_mine)
    kv_at = (kv_far, kv_far + first[0])
    qg_at = (qg_far + second[1], qg_far)
    pick = lambda at, flip: jnp.where((yy == 0) != flip, at[0], at[1]).astype(BF)
    kv_own, kv_give = pick(kv_at, False), pick(kv_at, True)
    qg_own, qg_give = pick(qg_at, False), pick(qg_at, True)

    qg_got = [[qg_own, hand(qg_give, 0, 2)]]
    for d in range(1, parts):
        qg_got.append([hand(qg_own, d, 0), hand(qg_give, d, 2)])
    kv_got = [kv_own, hand(kv_give, 0, 2)]
    kv_far4 = kv_got + [swap(a, 1) for a in kv_got]
    qg_far4 = [g + [swap(a, 1) for a in g] for g in qg_got]

    features = w_value.shape[0]
    outs = pl.pallas_call(
        functools.partial(finish, parts),
        out_shape=(st(rows, width),) * 3 + (st(rows, features),),
        in_specs=[SMEM] + [VMEM] * (7 + 2 * (parts - 1) + 4 + 4 * parts),
        out_specs=[HBM] * 4,
        scratch_shapes=[
            pltpu.VMEM((rows, parts * width), BF),
            pltpu.VMEM((rows, width), BF),
            pltpu.VMEM((rows, width), BF),
            pltpu.VMEM((rows, width), BF),
            pltpu.VMEM((rows, features), BF),
            pltpu.SemaphoreType.DMA((3 + max(1, features // 512),)),
        ],
        name="finish",
        cost_estimate=pl.CostEstimate(
            flops=2 * rows * features * parts * width, bytes_accessed=2 * features * parts * width, transcendentals=0
        ),
    )(
        pos, key, value, sensitivity, dq, dk, dv, w_value,
        *[a for pair in zip(key_others, dv_others) for a in pair],
        *kv_far4,
        *[a for g in qg_far4 for a in g],
    )
    return outs


def solution(mesh):
    spec = P("seq", "head")
    return jax.shard_map(
        per_device,
        mesh=mesh,
        in_specs=(spec, spec, spec, spec, P("head", None)),
        out_specs=(spec,) * 4,
        check_vma=False,
    )
```

```python
import functools

import jax
import jax.numpy as jnp
from jax import lax
from jax.experimental import pallas as pl
from jax.experimental.pallas import tpu as pltpu
from jax.sharding import PartitionSpec as P

DH = 128
PLANE = 4
BF = jnp.bfloat16
F32 = jnp.float32


def dot(a, b, ca, cb):
    return lax.dot_general(a, b, (((ca,), (cb,)), ((), ())), preferred_element_type=F32)


def cols(h):
    if isinstance(h, int):
        return slice(h * DH, (h + 1) * DH)
    return pl.ds(pl.multiple_of(h * DH, DH), DH)


def place():
    seq = lax.axis_index("seq")
    return lax.rem(seq, 2), lax.rem(seq // 2, 2), seq // PLANE


def call(kernel, name, outs, near=(), far=(), scratch=(), flops=0, nbytes=0, out_space=pltpu.VMEM, limit=4 << 20):
    return pl.pallas_call(
        kernel,
        out_shape=[out_space(s, d) for s, d in outs],
        in_specs=[pl.BlockSpec(memory_space=pltpu.VMEM)] * len(near) + [pl.BlockSpec(memory_space=pltpu.HBM)] * len(far),
        out_specs=[pl.BlockSpec(memory_space=out_space)] * len(outs),
        scratch_shapes=list(scratch),
        name=name,
        compiler_params=pltpu.CompilerParams(vmem_limit_bytes=limit),
        cost_estimate=pl.CostEstimate(flops=flops, bytes_accessed=nbytes, transcendentals=0),
    )(
        *[pltpu.with_memory_space_constraint(a, pltpu.VMEM) for a in near],
        *[pltpu.with_memory_space_constraint(a, pltpu.HBM) for a in far],
    )


def local_states(q_hbm, k_hbm, v_hbm, g_hbm, keep_ref, give_ref, extra_ref, q_ref, k_ref, v_ref, g_ref, sem):
    loads = [
        pltpu.make_async_copy(a, b, sem.at[i])
        for i, (a, b) in enumerate(((q_hbm, q_ref), (g_hbm, g_ref), (k_hbm, k_ref), (v_hbm, v_ref)))
    ]
    for load in loads:
        load.start()
    core = place()[0]
    half = keep_ref.shape[1]
    for load in loads:
        load.wait()
    for j in range(half):
        for owner, out in ((1 - core, give_ref), (core, keep_ref)):
            at = cols(owner * half + j)
            qg = dot(q_ref[:, at], g_ref[:, at], 0, 0)
            kv = dot(k_ref[:, at], v_ref[:, at], 0, 0)
            out[0, j] = kv.astype(out.dtype)
            out[1, j] = qg.astype(out.dtype)
        extra_ref[j] = jnp.where(core == 0, kv, qg).astype(BF)


def chip_sum(keep_ref, got_ref, mine_ref, give_ref):
    yy = place()[1]
    quarter = mine_ref.shape[1]
    for i in range(2):
        for j in range(quarter):
            a, b = yy * quarter + j, (1 - yy) * quarter + j
            mine_ref[i, j] = keep_ref[i, a] + got_ref[i, a].astype(F32)
            give_ref[i, j] = (keep_ref[i, b] + got_ref[i, b].astype(F32)).astype(BF)


def inside_block(q_ref, k_ref, v_ref, g_ref, got_ref, extra_ref, w_hbm, dq_ref, dk_ref, dv_ref, sent_ref, w_ref, sem):
    load = pltpu.make_async_copy(w_hbm, w_ref, sem)
    load.start()
    core = place()[0]
    rows = q_ref.shape[0]
    half = extra_ref.shape[0]
    t = lax.broadcasted_iota(jnp.int32, (rows, rows), 0)
    s = lax.broadcasted_iota(jnp.int32, (rows, rows), 1)
    causal = s <= t
    for j in range(half):
        for owner in (core, 1 - core):
            at = cols(owner * half + j)
            state = got_ref[1 - core, j] if owner is core else extra_ref[j]
            q, k, v, g = q_ref[:, at], k_ref[:, at], v_ref[:, at], g_ref[:, at]
            kv = jnp.where(core == 1, state, jnp.zeros_like(state))
            qg = jnp.where(core == 0, state, jnp.zeros_like(state))
            scores = jnp.where(causal, dot(q, k, 1, 1), 0.0).astype(BF)
            grads = jnp.where(causal, dot(g, v, 1, 1), 0.0).astype(BF)
            dq_ref[:, at] = dot(grads, k, 1, 0) + dot(g, kv, 1, 1)
            dk_ref[:, at] = dot(grads, q, 0, 0) + dot(v, qg, 1, 1)
            dv = dot(scores, g, 0, 0) + dot(k, qg, 1, 0)
            dv_ref[:, at] = dv
            sent_ref[:, at] = dv.astype(BF)
    load.wait()


def plane_sum(mine_ref, other_ref, *sent_refs):
    zz = place()[2]
    both = [mine_ref[i] + other_ref[i].astype(F32) for i in range(2)]
    for d, sent in enumerate(sent_refs, 1):
        sent[...] = jnp.where((zz ^ d) > zz, both[0], both[1]).astype(BF)


def plane_total(mine_ref, other_ref, kv_ref, qg_ref):
    kv_ref[...] = mine_ref[0] + other_ref[0].astype(F32)
    qg_ref[...] = mine_ref[1] + other_ref[1].astype(F32)


def far_states(mine_ref, other_ref, *refs):
    own_ref, give_ref, qg_own_ref, qg_give_ref = refs[-4:]
    got = refs[:-4]
    _, yy, zz = place()
    if got[0].dtype == F32:
        kv, qg = got[0][...], got[1][...]
    else:
        kv = qg = jnp.zeros(got[0].shape, F32)
        for d, ref in enumerate(got, 1):
            a = ref[...].astype(F32)
            below = (zz ^ d) < zz
            kv = kv + jnp.where(below, a, 0.0)
            qg = qg + jnp.where(below, 0.0, a)
    first = yy == 0
    kv_own = jnp.where(first, kv, kv + other_ref[0].astype(F32))
    kv_give = jnp.where(first, kv + mine_ref[0], kv)
    qg_own = jnp.where(first, qg + other_ref[1].astype(F32), qg).astype(BF)
    qg_give = jnp.where(first, qg, qg + mine_ref[1]).astype(BF)
    own_ref[0], own_ref[1] = kv_own.astype(BF), qg_own
    give_ref[0], give_ref[1] = kv_give.astype(BF), qg_give
    qg_own_ref[...], qg_give_ref[...] = qg_own, qg_give


def finish(parts, *refs):
    k_ref, v_ref, g_ref, dq_ref, dk_ref, dv_ref, w_ref = refs[:7]
    own = refs[7:11]
    others = [refs[11 + 6 * i : 17 + 6 * i] for i in range(parts - 1)]
    qo, ko, vo, io, full, qs, ks, vs, os, sem = refs[11 + 6 * (parts - 1) :]
    core, yy, _ = place()
    x = lax.axis_index("head")
    quarter = own[0].shape[1]
    width = k_ref.shape[1]
    quarters = [((core + piece // 2) % 2 * 2 + (yy + piece % 2) % 2) * quarter for piece in range(4)]
    for i in range(parts):
        x_from = lax.rem(x - i + parts, parts)
        kk, base = (k_ref, dv_ref) if i == 0 else others[i - 1][:2]
        for piece, first in enumerate(quarters):
            for j in range(quarter):
                at = cols(first + j)
                state = own[piece][1, j] if i == 0 else others[i - 1][2 + piece][j]
                dv = (base[:, at].astype(F32) + dot(kk[:, at], state, 1, 0)).astype(BF)
                full[:, pl.ds(pl.multiple_of(x_from * width + (first + j) * DH, DH), DH)] = dv
                if i == 0:
                    vs[:, at] = dv
    copies = []

    def out(a, b):
        copies.append(pltpu.make_async_copy(a, b, sem.at[len(copies)]))
        copies[-1].start()

    out(vs, vo)
    features = w_ref.shape[0]
    step = min(512, features)
    for f in range(0, features, step):
        os[:, f : f + step] = dot(full[...], w_ref[f : f + step, :], 1, 1).astype(BF)
        out(os.at[:, f : f + step], io.at[:, f : f + step])
    for piece, first in enumerate(quarters):
        for j in range(quarter):
            at = cols(first + j)
            ks[:, at] = (dk_ref[:, at] + dot(v_ref[:, at], own[piece][1, j], 1, 1)).astype(BF)
            qs[:, at] = (dq_ref[:, at] + dot(g_ref[:, at], own[piece][0, j], 1, 1)).astype(BF)
    out(ks, ko)
    out(qs, qo)
    for copy in copies:
        copy.wait()


def swap(value, bit):
    n = lax.axis_size("seq")
    return lax.ppermute(value, "seq", [(i, i ^ bit) for i in range(n)])


def hand(value, dx, bit):
    n, m = lax.axis_size("seq"), lax.axis_size("head")
    pairs = [(s * m + x, (s ^ bit) * m + (x + dx) % m) for s in range(n) for x in range(m)]
    return lax.ppermute(value, ("seq", "head"), pairs)


def across_planes(mine, other):
    n = lax.axis_size("seq")
    planes = n // PLANE
    one = mine.shape[1:]
    if planes & (planes - 1) == 0 and planes - 1 <= 2 * (planes - 1).bit_length():
        sent = call(plane_sum, "plane_sum", [(one, BF)] * (planes - 1), near=(mine, other))
        return [swap(a, d * PLANE) for d, a in enumerate(sent, 1)]
    kv, qg = call(plane_total, "plane_total", [(one, F32)] * 2, near=(mine, other))

    def up(a, by):
        return lax.ppermute(a.astype(BF), "seq", [(i, i + by) for i in range(n - by)]).astype(F32)

    def down(a, by):
        return lax.ppermute(a.astype(BF), "seq", [(i + by, i) for i in range(n - by)]).astype(F32)

    kv, qg = up(kv, PLANE), down(qg, PLANE)
    reach = 1
    while reach < planes:
        kv, qg = kv + up(kv, reach * PLANE), qg + down(qg, reach * PLANE)
        reach *= 2
    return [kv, qg]


def per_device(query, key, value, sensitivity, w_value):
    rows, width = query.shape
    heads = width // DH
    half, quarter = heads // 2, heads // 4
    features = w_value.shape[0]
    parts = lax.axis_size("head")
    tile = (DH, DH)
    flat = (rows, width)
    mm = 2 * rows * DH * DH

    keep, give, extra, query, key, value, sensitivity = call(
        local_states,
        "local_states",
        [((2, half) + tile, F32), ((2, half) + tile, BF), ((half,) + tile, BF)] + [(flat, BF)] * 4,
        far=(query, key, value, sensitivity),
        scratch=[pltpu.SemaphoreType.DMA((4,))],
        flops=2 * heads * mm,
        nbytes=8 * rows * width,
    )
    got = swap(give, 1)
    extra = swap(extra, 1)
    mine, give = call(chip_sum, "chip_sum", [((2, quarter) + tile, F32), ((2, quarter) + tile, BF)], near=(keep, got))
    other = swap(give, 2)
    key_others = [hand(key, d, 0) for d in range(1, parts)]

    dq, dk, dv, dv16, w_near = call(
        inside_block,
        "inside_block",
        [(flat, F32)] * 3 + [(flat, BF), (w_value.shape, BF)],
        near=(query, key, value, sensitivity, got, extra),
        far=(w_value,),
        scratch=[pltpu.SemaphoreType.DMA],
        flops=8 * heads * mm,
        nbytes=2 * w_value.size,
    )
    other, dv16 = lax.optimization_barrier((other, dv16))
    dv_others = [hand(dv16, d, 0) for d in range(1, parts)]

    arrived = across_planes(mine, other)
    own, give, qg_own, qg_give = call(
        far_states,
        "far_states",
        [((2, quarter) + tile, BF)] * 2 + [((quarter,) + tile, BF)] * 2,
        near=(mine, other, *arrived),
    )
    beside = [[hand(qg_own, d, 0), hand(qg_give, d, 2)] for d in range(1, parts)]
    both = [own, hand(give, 0, 2)]
    both = both + [swap(a, 1) for a in both]
    beside = [b + [swap(a, 1) for a in b] for b in beside]

    return call(
        functools.partial(finish, parts),
        "finish",
        [(flat, BF)] * 3 + [((rows, features), BF)],
        near=(
            key, value, sensitivity, dq, dk, dv, w_near, *both,
            *[a for k, d, b in zip(key_others, dv_others, beside) for a in (k, d, *b)],
        ),
        scratch=[
            pltpu.VMEM((rows, parts * width), BF),
            pltpu.VMEM(flat, BF),
            pltpu.VMEM(flat, BF),
            pltpu.VMEM(flat, BF),
            pltpu.VMEM((rows, features), BF),
            pltpu.SemaphoreType.DMA((3 + max(1, features // 512),)),
        ],
        out_space=pltpu.HBM,
        limit=8 << 20,
        flops=2 * rows * features * parts * width,
        nbytes=2 * features * parts * width,
    )


def solution(mesh):
    spec = P("seq", "head")
    return jax.shard_map(
        per_device,
        mesh=mesh,
        in_specs=(spec, spec, spec, spec, P("head", None)),
        out_specs=(spec,) * 4,
        check_vma=False,
    )
```
